1024 devices in a mesh: dp: 16 (over x_lo, y, core), seq: 64 (over x_hi, z).
Axes of the slice: x: 4 (x_hi: 2, x_lo: 2; x = x_hi * 2 + x_lo), y: 4, z: 32, core: 2. Of those that a mesh axis runs over, the one named last changes fastest.
Arguments:
- inputs: bfloat16 [16, 12288, 768], P('dp', 'seq'), may hold values from -6 to 6
- cotangent: bfloat16 [16, 12288, 768], P('dp', 'seq'), may hold values from -16 to 16
- dilated_kernel_weight: bfloat16 [768, 3, 384], P('dp'), may hold values from -0.125 to 0.125
- point_weight: bfloat16 [384, 768], P('dp'), may hold values from -0.3125 to 0.3125
Outputs:
- grad_input: bfloat16 [16, 12288, 768], P('dp', 'seq')
- kernel_weight_gradient: float32 [768, 3, 384], P('dp')
- pointwise_weight_gradient: float32 [384, 768], P('dp')
The draws below stay inside these ranges and needn't reach their ends.
All inputs are finite; a program needn't handle non-finite values.
Results may differ from the reference program's by a relative error of at most 0.0054.
Values may be sent and summed in bfloat16 or wider, within the bound.
No kernel may reach another device: no remote copies, remote signals or barrier semaphores. Data moves between devices by JAX's collectives and lax.ppermute only.
A program may use at most 32 MiB of HBM per device.

```python
import jax
import jax.numpy as jnp
from jax import lax

C = 768
CI = 384
DILATION_SPAN = 32
SEQS = 16
BINS = 12288


def strengthened(entries, key, source, target, parts, factor):
    def block_of(dim):
        return (jnp.arange(entries.shape[dim]) // (entries.shape[dim] // parts)).reshape((-1,) + (1,) * (entries.ndim - 1 - dim))

    near = jax.random.permutation(key, parts)[block_of(target)]
    other_side = (block_of(target) + parts // 2) % parts
    return jnp.where((block_of(source) == near) | (block_of(source) == other_side), factor * entries, entries)


def levels(key, dims, cuts, least, high):
    factor_of, own = 1.0, jax.random.fold_in(key, 6)
    for position, blocks in cuts:
        draws = jnp.exp(jax.random.uniform(jax.random.fold_in(own, position), (blocks,), jnp.float32, least / len(cuts), high / len(cuts)))
        factor_of = factor_of * jnp.repeat(draws, dims[position] // blocks).reshape([-1 if axis == position else 1 for axis in range(len(dims))])
    return factor_of


def centred(stream_key, extent, width, limit, pieces=(), kind=jnp.bfloat16):
    entries = width * jax.random.normal(stream_key, extent, jnp.float32)
    if pieces:
        entries = entries * levels(stream_key, extent, pieces, -0.22, 0.18)
    return jnp.clip(entries, -limit, limit).astype(kind)


def gaussian_with(stream_key, dims, deviation, most, cuts, heavy, dtype=jnp.bfloat16):
    result = deviation * jax.random.normal(stream_key, dims, jnp.float32)
    if cuts:
        result = result * levels(stream_key, dims, cuts, -0.22, 0.18)
    return jnp.clip(strengthened(result, jax.random.fold_in(stream_key, 3), *heavy), -most, most).astype(dtype)


def setup_inputs(seed: int = 0) -> dict:
    seeds = jax.random.split(jax.random.key(seed), 5)
    inputs = centred(seeds[0], (SEQS, BINS, C), 1.0, 6.0, ((0, 16), (1, 64)))
    cotangent = gaussian_with(seeds[1], (SEQS, BINS, C), 1.0, 16.0, ((0, 16), (1, 64)), (1, 2, 64, 4.0))
    dilated_kernel_weight = centred(seeds[2], (C, 3, CI), (3 * C) ** -0.5, 0.125, ((0, 16),))
    point_weight = centred(seeds[3], (CI, C), CI ** -0.5, 0.3125, ((0, 16),))
    return dict(inputs=inputs, cotangent=cotangent, dilated_kernel_weight=dilated_kernel_weight, point_weight=point_weight)


def gelu_apply(values):
    return jax.nn.gelu(values, approximate=True)

def rms_normed(values):
    return values * lax.rsqrt(lax.optimization_barrier(jnp.mean(values * values, axis=-1, keepdims=True)) + 1e-06)

def reference(inputs, cotangent, dilated_kernel_weight, point_weight):

    def per_sequence(totals, sample_pair):
        seq_inputs, seq_cot = sample_pair
        input_length = seq_inputs.shape[0]
        normal, pull_norm = jax.vjp(rms_normed, seq_inputs.astype(jnp.float32))
        activated_hidden, pull_act = jax.vjp(gelu_apply, normal)
        padded_activation = jnp.pad(activated_hidden.astype(jnp.bfloat16), ((DILATION_SPAN, DILATION_SPAN), (0, 0)))
        preactivation = sum((jnp.dot(padded_activation[kernel_tap_index * DILATION_SPAN:kernel_tap_index * DILATION_SPAN + input_length], dilated_kernel_weight[:, kernel_tap_index, :], preferred_element_type=jnp.float32) for kernel_tap_index in range(3)))
        hidden, pull_hidden = jax.vjp(gelu_apply, preactivation)
        hidden_halfprec = hidden.astype(jnp.bfloat16)
        pointwise_weight_gradient = jnp.dot(hidden_halfprec.T, seq_cot, preferred_element_type=jnp.float32)
        upstream_gradient = jnp.dot(seq_cot, point_weight.T, preferred_element_type=jnp.float32)
        delta_rows = pull_hidden(upstream_gradient)[0].astype(jnp.bfloat16)
        kernel_weight_gradient = jnp.stack([jnp.dot(padded_activation[kernel_tap_index * DILATION_SPAN:kernel_tap_index * DILATION_SPAN + input_length].T, delta_rows, preferred_element_type=jnp.float32) for kernel_tap_index in range(3)], axis=1)
        padded_delta = jnp.pad(delta_rows, ((DILATION_SPAN, DILATION_SPAN), (0, 0)))
        activation_gradient = sum((jnp.dot(padded_delta[(2 - kernel_tap_index) * DILATION_SPAN:(2 - kernel_tap_index) * DILATION_SPAN + input_length], dilated_kernel_weight[:, kernel_tap_index, :].T, preferred_element_type=jnp.float32) for kernel_tap_index in range(3)))
        grad_normal = pull_act(activation_gradient)[0]
        grad_inner = pull_norm(grad_normal)[0]
        grad_input = (seq_cot.astype(jnp.float32) + grad_inner).astype(jnp.bfloat16)
        return ((totals[0] + kernel_weight_gradient, totals[1] + pointwise_weight_gradient), grad_input)
    start = (jnp.zeros(dilated_kernel_weight.shape, jnp.float32), jnp.zeros(point_weight.shape, jnp.float32))
    (kernel_weight_gradient, pointwise_weight_gradient), grad_input = lax.scan(per_sequence, start, (inputs, cotangent))
    return (grad_input, kernel_weight_gradient, pointwise_weight_gradient)
```

```python
import jax
import jax.numpy as jnp
from jax import lax
from jax.experimental import pallas as pl
from jax.experimental.pallas import tpu as pltpu
from jax.sharding import Mesh
from jax.sharding import PartitionSpec as P


SPAN = 32
EPS = 1e-06
ALPHA = 0.7978845608028654
BETA = 0.044715
ZL = 2
DP = ("xl", "y", "c")
SEQ = ("xh", "zh", "zl")
PAIR = [(0, 1), (1, 0)]
BF16, F32 = jnp.bfloat16, jnp.float32


def dot(a, b, ca, cb):
    return lax.dot_general(a, b, (((ca,), (cb,)), ((), ())), preferred_element_type=F32)


def gelu_value(v):
    return 0.5 * v * (1.0 + jnp.tanh(ALPHA * (v + BETA * (v * v * v))))


def gelu_both(v):
    t = jnp.tanh(ALPHA * (v + BETA * (v * v * v)))
    half = 0.5 * (1.0 + t)
    slope = half + 0.5 * v * (1.0 - t * t) * (ALPHA * (1.0 + 3.0 * BETA * (v * v)))
    return v * half, slope


def inverse_rms(x):
    return lax.rsqrt(jnp.mean(x * x, axis=-1, keepdims=True) + EPS)


def pack_body(wk, wp, xa, xb, ca, cb, copies, up, down):
    taps, rows, ci = wk.shape
    w = [wk[k] for k in range(taps)]
    p = wp[...].astype(F32)
    p = jnp.concatenate([p[:, :ci], p[:, ci:]], axis=0).astype(BF16)
    for i in range(copies.shape[0]):
        for k in range(taps):
            copies[i, k * rows : (k + 1) * rows] = w[k]
        copies[i, taps * rows :] = p
    up[: 2 * SPAN] = xb[...]
    up[2 * SPAN :] = cb[...]
    down[: 2 * SPAN] = xa[...]
    down[2 * SPAN :] = ca[...]


def act_body(x, cot, before, after, act, wide):
    n, h = x.shape[0], 2 * SPAN

    def part(v):
        v = v.astype(F32)
        return gelu_value(v * inverse_rms(v)).astype(BF16)

    act[:h] = part(before[:h])
    act[h : h + n] = part(x[...])
    act[h + n :] = part(after[:h])
    wide[:SPAN] = before[h:]
    wide[SPAN : SPAN + n] = cot[...]
    wide[SPAN + n :] = after[h:]


def main_body(c_ref, near, far, act, wide, delta, wk, mine, send, wp_s, dk_s, dp_s):
    c = c_ref[0]
    groups, _, ci = near.shape
    taps, channels, _ = wk.shape
    rows, prow = channels // (2 * groups), ci // (2 * groups)
    m = wide.shape[0]
    n = m - 2 * SPAN
    for ref, core in ((near, c), (far, 1 - c)):
        for i in range(groups):
            d = 2 * i + core
            for k in range(taps):
                wk[k, pl.ds(pl.multiple_of(d * rows, rows), rows)] = ref[i, k * rows : (k + 1) * rows]
            p = ref[i, taps * rows :].astype(F32)
            at = pl.ds(pl.multiple_of(d * prow, prow), prow)
            wp_s[at, :ci] = p[:prow]
            wp_s[at, ci:] = p[prow:]
    preact = dot(act[:m], wk[0], 1, 0)
    for k in range(1, taps):
        preact = preact + dot(act[k * SPAN : k * SPAN + m], wk[k], 1, 0)
    hidden, slope = gelu_both(preact)
    upstream = dot(wide[...], wp_s[...].astype(BF16), 1, 1)
    deltas = (upstream * slope).astype(BF16)
    delta[...] = deltas
    dp_s[...] = dot(hidden[SPAN : SPAN + n].astype(BF16), wide[SPAN : SPAN + n], 0, 0)
    inner = deltas[SPAN : SPAN + n]
    for k in range(taps):
        dk_s[k] = dot(act[(k + 1) * SPAN : (k + 1) * SPAN + n], inner, 0, 0)
    for ref, core in ((mine, c), (send, 1 - c)):
        for i in range(groups):
            d = 2 * i + core
            for k in range(taps):
                v = dk_s[k, pl.ds(pl.multiple_of(d * rows, rows), rows)]
                ref[i, k * rows : (k + 1) * rows] = v.astype(ref.dtype)
            at = pl.ds(pl.multiple_of(d * prow, prow), prow)
            v = jnp.concatenate([dp_s[at, :ci], dp_s[at, ci:]], axis=0)
            ref[i, taps * rows :] = v.astype(ref.dtype)


def input_body(delta, wk, x, cot, out):
    taps, n = wk.shape[0], x.shape[0]
    grad = dot(delta[(taps - 1) * SPAN : (taps - 1) * SPAN + n], wk[0], 1, 1)
    for k in range(1, taps):
        at = (taps - 1 - k) * SPAN
        grad = grad + dot(delta[at : at + n], wk[k], 1, 1)
    v = x[...].astype(F32)
    r = inverse_rms(v)
    _, slope = gelu_both(v * r)
    g = grad * slope
    inner = r * g - v * (r * r * r * jnp.mean(v * g, axis=-1, keepdims=True))
    out[...] = (cot[...].astype(F32) + inner).astype(BF16)


def sds(shape, dtype):
    return jax.ShapeDtypeStruct(shape, dtype)


def in_hbm(a):
    return pltpu.with_memory_space_constraint(a, pltpu.HBM)


def limit(mib):
    return pltpu.CompilerParams(vmem_limit_bytes=mib << 20)


def copies_to(x, axis):
    n = lax.axis_size(axis)
    y = jnp.broadcast_to(x[None], (n,) + x.shape).reshape((n * x.shape[0],) + x.shape[1:])
    return lax.all_to_all(y, axis, 0, 0, tiled=True)


def exchanged_sum(x, axis):
    n = lax.axis_size(axis)
    y = lax.all_to_all(x, axis, 0, 0, tiled=True)
    return jnp.sum(y.reshape((n, x.shape[0] // n) + x.shape[1:]).astype(F32), axis=0)


def per_device(inputs, cotangent, dilated_kernel_weight, point_weight):
    x, cot = inputs[0], cotangent[0]
    n, C = x.shape
    rows, taps, CI = dilated_kernel_weight.shape
    prow = point_weight.shape[0]
    total = taps * rows + 2 * prow
    groups = lax.axis_size("xl") * lax.axis_size("y")
    seq = lax.axis_size(SEQ)
    core = lax.axis_index("c")
    h = 2 * SPAN
    whole = lambda *s: pl.BlockSpec(s, lambda *_: (0,) * len(s))

    last = n // h - 1
    edge = n // SPAN - 1
    copies, up, down = pl.pallas_call(
        pack_body,
        grid=(1,),
        in_specs=[
            whole(taps, rows, CI),
            whole(prow, C),
            pl.BlockSpec((h, C), lambda i: (0, 0)),
            pl.BlockSpec((h, C), lambda i: (last, 0)),
            pl.BlockSpec((SPAN, C), lambda i: (0, 0)),
            pl.BlockSpec((SPAN, C), lambda i: (edge, 0)),
        ],
        out_specs=[whole(groups, total, CI), whole(h + SPAN, C), whole(h + SPAN, C)],
        out_shape=[sds((groups, total, CI), BF16), sds((h + SPAN, C), BF16), sds((h + SPAN, C), BF16)],
        name="pack",
        compiler_params=limit(14),
    )(*map(in_hbm, (jnp.swapaxes(dilated_kernel_weight, 0, 1), point_weight, x, x, cot, cot)))

    after = lax.ppermute(down, SEQ, [(i + 1, i) for i in range(seq - 1)])
    before = lax.ppermute(up, SEQ, [(i, i + 1) for i in range(seq - 1)])
    near = lax.all_to_all(copies.reshape(groups * total, CI), ("xl", "y"), 0, 0, tiled=True)
    far = lax.ppermute(near, "c", PAIR)
    near, far = near.reshape(groups, total, CI), far.reshape(groups, total, CI)

    spec = pl.BlockSpec(memory_space=pltpu.VMEM)
    far = in_hbm(far)
    act, wide = pl.pallas_call(
        act_body,
        in_specs=[spec] * 4,
        out_specs=[spec] * 2,
        out_shape=[sds((n + 2 * h, C), BF16), sds((n + h, C), BF16)],
        name="act",
        compiler_params=limit(14),
    )(x, cot, before, after)
    delta, wk, mine, send = pl.pallas_call(
        main_body,
        in_specs=[pl.BlockSpec(memory_space=pltpu.SMEM)] + [spec] * 4,
        out_specs=[spec] * 4,
        out_shape=[
            sds((n + h, CI), BF16),
            sds((taps, C, CI), BF16),
            sds((groups, total, CI), F32),
            sds((groups, total, CI), BF16),
        ],
        scratch_shapes=[
            pltpu.VMEM((CI, C), F32),
            pltpu.VMEM((taps, C, CI), F32),
            pltpu.VMEM((CI, C), F32),
        ],
        name="main",
        compiler_params=limit(14),
    )(core.reshape(1).astype(jnp.int32), near, far, act, wide)
    got = lax.ppermute(send, "c", PAIR)
    grad_input = pl.pallas_call(input_body, in_specs=[spec] * 4, out_shape=sds((n, C), BF16), name="input_grad", compiler_params=limit(14))(delta, wk, x, cot)

    s = (mine + got.astype(F32)).astype(BF16).reshape(groups * total, CI)
    s = exchanged_sum(s, ("xl", "y", "xh"))
    s = exchanged_sum(s, "zl")
    s = jnp.sum(lax.all_gather(s.astype(BF16), "zh", axis=0).astype(F32), axis=0)
    s = copies_to(s, ("xh", "zl"))
    owned_conv = jnp.swapaxes(s[: taps * rows].reshape(taps, rows, CI), 0, 1)
    q = taps * rows
    owned_point = jnp.concatenate([s[q : q + prow], s[q + prow :]], axis=1)
    return (grad_input[None], owned_conv, owned_point)


def solution(mesh):
    fine = Mesh(mesh.devices.reshape(2, 4, 2, 2, 32 // ZL, ZL), DP + SEQ)
    return jax.shard_map(
        per_device,
        mesh=fine,
        in_specs=(P(DP, SEQ, None), P(DP, SEQ, None), P(DP, None, None), P(DP, None)),
        out_specs=(P(DP, SEQ, None), P(DP, None, None), P(DP, None)),
        check_vma=False,
    )
```

```python
import jax
import jax.numpy as jnp
from jax import lax
from jax.experimental import pallas as pl
from jax.experimental.pallas import tpu as pltpu
from jax.sharding import Mesh
from jax.sharding import PartitionSpec as P


SPAN = 32
EPS = 1e-06
ALPHA = 0.7978845608028654
BETA = 0.044715
ZL = 2
DP = ("xl", "y", "c")
SEQ = ("xh", "zh", "zl")
PAIR = [(0, 1), (1, 0)]
BF16, F32 = jnp.bfloat16, jnp.float32


def dot(a, b, ca, cb):
    return lax.dot_general(a, b, (((ca,), (cb,)), ((), ())), preferred_element_type=F32)


def gelu_value(v):
    return 0.5 * v * (1.0 + jnp.tanh(ALPHA * (v + BETA * (v * v * v))))


def gelu_both(v):
    t = jnp.tanh(ALPHA * (v + BETA * (v * v * v)))
    half = 0.5 * (1.0 + t)
    slope = half + 0.5 * v * (1.0 - t * t) * (ALPHA * (1.0 + 3.0 * BETA * (v * v)))
    return v * half, slope


def inverse_rms(x):
    return lax.rsqrt(jnp.mean(x * x, axis=-1, keepdims=True) + EPS)


def pack_body(wk, wp, xa, xb, ca, cb, copies, up, down):
    taps, rows, ci = wk.shape
    w = [wk[k] for k in range(taps)]
    p = wp[...].astype(F32)
    p = jnp.concatenate([p[:, :ci], p[:, ci:]], axis=0).astype(BF16)
    for i in range(copies.shape[0]):
        for k in range(taps):
            copies[i, k * rows : (k + 1) * rows] = w[k]
        copies[i, taps * rows :] = p
    up[: 2 * SPAN] = xb[...]
    up[2 * SPAN :] = cb[...]
    down[: 2 * SPAN] = xa[...]
    down[2 * SPAN :] = ca[...]


def act_body(x, cot, before, after, act, wide):
    n, h = x.shape[0], 2 * SPAN

    def part(v):
        v = v.astype(F32)
        return gelu_value(v * inverse_rms(v)).astype(BF16)

    act[:h] = part(before[:h])
    act[h : h + n] = part(x[...])
    act[h + n :] = part(after[:h])
    wide[:SPAN] = before[h:]
    wide[SPAN : SPAN + n] = cot[...]
    wide[SPAN + n :] = after[h:]


def main_body(c_ref, near, far, act, wide, delta, wk, mine, send, wp_s):
    c = c_ref[0]
    groups, _, ci = near.shape
    taps, channels, _ = wk.shape
    rows, prow = channels // (2 * groups), ci // (2 * groups)
    m = wide.shape[0]
    n = m - 2 * SPAN
    for ref, core in ((near, c), (far, 1 - c)):
        for i in range(groups):
            d = 2 * i + core
            for k in range(taps):
                wk[k, pl.ds(pl.multiple_of(d * rows, rows), rows)] = ref[i, k * rows : (k + 1) * rows]
            p = ref[i, taps * rows :].astype(F32)
            at = pl.ds(pl.multiple_of(d * prow, prow), prow)
            wp_s[at, :ci] = p[:prow]
            wp_s[at, ci:] = p[prow:]
    preact = dot(act[:m], wk[0], 1, 0)
    for k in range(1, taps):
        preact = preact + dot(act[k * SPAN : k * SPAN + m], wk[k], 1, 0)
    hidden, slope = gelu_both(preact)
    upstream = dot(wide[...], wp_s[...].astype(BF16), 1, 1)
    deltas = (upstream * slope).astype(BF16)
    delta[...] = deltas
    inner = deltas[SPAN : SPAN + n]

    def place(v, at, pieces):
        count = v.shape[0] // (2 * groups)
        for core in range(2):

            @pl.when(c == core)
            def _():
                for i in range(groups):
                    own, other = (2 * i + core) * count, (2 * i + 1 - core) * count
                    mine[i, at : at + pieces * count] = halves(v[own : own + count], pieces)
                    send[i, at : at + pieces * count] = halves(v[other : other + count], pieces).astype(BF16)

    place(dot(hidden[SPAN : SPAN + n].astype(BF16), wide[SPAN : SPAN + n], 0, 0), taps * rows, 2)
    for k in range(taps):
        place(dot(act[(k + 1) * SPAN : (k + 1) * SPAN + n], inner, 0, 0), k * rows, 1)


def halves(v, pieces):
    width = v.shape[1] // pieces
    return jnp.concatenate([v[:, k * width : (k + 1) * width] for k in range(pieces)], axis=0)


def spread_body(parts, copies):
    total = jnp.sum(parts[...].astype(F32), axis=0)
    for i in range(copies.shape[0]):
        copies[i] = total


def finish_body(s, conv, point):
    taps, rows, ci = conv.shape
    for k in range(taps):
        conv[k] = s[k * rows : (k + 1) * rows]
    q, prow = taps * rows, point.shape[0]
    point[:, :ci] = s[q : q + prow]
    point[:, ci:] = s[q + prow :]


def input_body(delta, wk, _, x, cot, out):
    taps, n = wk.shape[0], x.shape[0]
    grad = dot(delta[(taps - 1) * SPAN : (taps - 1) * SPAN + n], wk[0], 1, 1)
    for k in range(1, taps):
        at = (taps - 1 - k) * SPAN
        grad = grad + dot(delta[at : at + n], wk[k], 1, 1)
    v = x[...].astype(F32)
    r = inverse_rms(v)
    _, slope = gelu_both(v * r)
    g = grad * slope
    inner = r * g - v * (r * r * r * jnp.mean(v * g, axis=-1, keepdims=True))
    out[...] = (cot[...].astype(F32) + inner).astype(BF16)


def sds(shape, dtype):
    return jax.ShapeDtypeStruct(shape, dtype)


def in_hbm(a):
    return pltpu.with_memory_space_constraint(a, pltpu.HBM)


def limit(mib):
    return pltpu.CompilerParams(vmem_limit_bytes=mib << 20)


def exchanged_sum(x, axis):
    n = lax.axis_size(axis)
    y = lax.all_to_all(x, axis, 0, 0, tiled=True)
    return jnp.sum(y.reshape((n, x.shape[0] // n) + x.shape[1:]).astype(F32), axis=0)


def per_device(inputs, cotangent, dilated_kernel_weight, point_weight):
    x, cot = inputs[0], cotangent[0]
    n, C = x.shape
    rows, taps, CI = dilated_kernel_weight.shape
    prow = point_weight.shape[0]
    total = taps * rows + 2 * prow
    groups = lax.axis_size("xl") * lax.axis_size("y")
    seq = lax.axis_size(SEQ)
    core = lax.axis_index("c")
    h = 2 * SPAN
    whole = lambda *s: pl.BlockSpec(s, lambda *_: (0,) * len(s))

    last = n // h - 1
    edge = n // SPAN - 1
    copies, up, down = pl.pallas_call(
        pack_body,
        grid=(1,),
        in_specs=[
            whole(taps, rows, CI),
            whole(prow, C),
            pl.BlockSpec((h, C), lambda i: (0, 0)),
            pl.BlockSpec((h, C), lambda i: (last, 0)),
            pl.BlockSpec((SPAN, C), lambda i: (0, 0)),
            pl.BlockSpec((SPAN, C), lambda i: (edge, 0)),
        ],
        out_specs=[whole(groups, total, CI), whole(h + SPAN, C), whole(h + SPAN, C)],
        out_shape=[sds((groups, total, CI), BF16), sds((h + SPAN, C), BF16), sds((h + SPAN, C), BF16)],
        name="pack",
        compiler_params=limit(2),
    )(*map(in_hbm, (jnp.swapaxes(dilated_kernel_weight, 0, 1), point_weight, x, x, cot, cot)))

    after = lax.ppermute(down, SEQ, [(i + 1, i) for i in range(seq - 1)])
    before = lax.ppermute(up, SEQ, [(i, i + 1) for i in range(seq - 1)])
    near = lax.all_to_all(copies.reshape(groups * total, CI), ("xl", "y"), 0, 0, tiled=True)
    far = lax.ppermute(near, "c", PAIR)
    near, far = near.reshape(groups, total, CI), far.reshape(groups, total, CI)

    spec = pl.BlockSpec(memory_space=pltpu.VMEM)
    act, wide = pl.pallas_call(
        act_body,
        in_specs=[spec] * 4,
        out_specs=[spec] * 2,
        out_shape=[sds((n + 2 * h, C), BF16), sds((n + h, C), BF16)],
        name="act",
        compiler_params=limit(2),
    )(x, cot, before, after)
    delta, wk, mine, send, spare = pl.pallas_call(
        main_body,
        in_specs=[pl.BlockSpec(memory_space=pltpu.SMEM)] + [spec] * 4,
        out_specs=[spec] * 5,
        out_shape=[
            sds((n + h, CI), BF16),
            sds((taps, C, CI), BF16),
            sds((groups, total, CI), F32),
            sds((groups, total, CI), BF16),
            sds((CI, C), F32),
        ],
        name="main",
        compiler_params=limit(2),
    )(core.reshape(1).astype(jnp.int32), near, far, act, wide)
    got = lax.ppermute(send, "c", PAIR)
    grad_input = pl.pallas_call(input_body, in_specs=[spec] * 5, out_shape=sds((n, C), BF16), name="input_grad", compiler_params=limit(2))(delta, wk, spare, x, cot)

    s = (mine + got.astype(F32)).astype(BF16).reshape(groups * total, CI)
    s = exchanged_sum(s, ("xl", "y", "xh", "zl"))
    parts = lax.all_gather(s.astype(BF16), "zh", axis=0)
    final = lax.axis_size("xh") * lax.axis_size("zl")
    own = s.shape[0]
    s = pl.pallas_call(
        spread_body,
        in_specs=[spec],
        out_specs=spec,
        out_shape=sds((final, own, CI), F32),
        name="spread",
        compiler_params=limit(2),
    )(parts)
    s = lax.all_to_all(s.reshape(final * own, CI), ("xh", "zl"), 0, 0, tiled=True)
    conv, owned_point = pl.pallas_call(
        finish_body,
        in_specs=[spec],
        out_specs=[spec] * 2,
        out_shape=[sds((taps, rows, CI), F32), sds((prow, C), F32)],
        name="finish",
        compiler_params=limit(2),
    )(s)
    owned_conv = jnp.swapaxes(conv, 0, 1)
    return (grad_input[None], owned_conv, owned_point)


def solution(mesh):
    fine = Mesh(mesh.devices.reshape(2, 4, 2, 2, 32 // ZL, ZL), DP + SEQ)
    return jax.shard_map(
        per_device,
        mesh=fine,
        in_specs=(P(DP, SEQ, None), P(DP, SEQ, None), P(DP, None, None), P(DP, None)),
        out_specs=(P(DP, SEQ, None), P(DP, None, None), P(DP, None)),
        check_vma=False,
    )
```

```python
import jax
import jax.numpy as jnp
from jax import lax
from jax.experimental import pallas as pl
from jax.experimental.pallas import tpu as pltpu
from jax.sharding import Mesh
from jax.sharding import PartitionSpec as P


SPAN = 32
EPS = 1e-06
ALPHA = 0.7978845608028654
BETA = 0.044715
ZL = 2
DP = ("xl", "y", "c")
SEQ = ("xh", "zh", "zl")
PAIR = [(0, 1), (1, 0)]
BF16, F32 = jnp.bfloat16, jnp.float32


def dot(a, b, ca, cb):
    return lax.dot_general(a, b, (((ca,), (cb,)), ((), ())), preferred_element_type=F32)


def gelu_value(v):
    return 0.5 * v * (1.0 + jnp.tanh(ALPHA * (v + BETA * (v * v * v))))


def gelu_both(v):
    t = jnp.tanh(ALPHA * (v + BETA * (v * v * v)))
    half = 0.5 * (1.0 + t)
    slope = half + 0.5 * v * (1.0 - t * t) * (ALPHA * (1.0 + 3.0 * BETA * (v * v)))
    return v * half, slope


def inverse_rms(x):
    return lax.rsqrt(jnp.mean(x * x, axis=-1, keepdims=True) + EPS)


def pack_body(wk, wp, xa, xb, ca, cb, copies, up, down):
    taps, rows, ci = wk.shape
    w = [wk[k] for k in range(taps)]
    p = wp[...].astype(F32)
    p = jnp.concatenate([p[:, :ci], p[:, ci:]], axis=0).astype(BF16)
    for i in range(copies.shape[0]):
        for k in range(taps):
            copies[i, k * rows : (k + 1) * rows] = w[k]
        copies[i, taps * rows :] = p
    up[: 2 * SPAN] = xb[...]
    up[2 * SPAN :] = cb[...]
    down[: 2 * SPAN] = xa[...]
    down[2 * SPAN :] = ca[...]


def settle_body(before, after, mark):
    mark[...] = before[...].astype(F32) + after[...].astype(F32)


def act_body(_, x, cot, before, after, act, wide):
    n, h = x.shape[0], 2 * SPAN

    def part(v):
        v = v.astype(F32)
        return gelu_value(v * inverse_rms(v)).astype(BF16)

    act[:h] = part(before[:h])
    act[h : h + n] = part(x[...])
    act[h + n :] = part(after[:h])
    wide[:SPAN] = before[h:]
    wide[SPAN : SPAN + n] = cot[...]
    wide[SPAN + n :] = after[h:]


def main_body(c_ref, near, far, act, wide, delta, wk, mine, send, wp_s):
    c = c_ref[0]
    groups, _, ci = near.shape
    taps, channels, _ = wk.shape
    rows, prow = channels // (2 * groups), ci // (2 * groups)
    m = wide.shape[0]
    n = m - 2 * SPAN
    for ref, core in ((near, c), (far, 1 - c)):
        for i in range(groups):
            d = 2 * i + core
            for k in range(taps):
                wk[k, pl.ds(pl.multiple_of(d * rows, rows), rows)] = ref[i, k * rows : (k + 1) * rows]
            p = ref[i, taps * rows :].astype(F32)
            at = pl.ds(pl.multiple_of(d * prow, prow), prow)
            wp_s[at, :ci] = p[:prow]
            wp_s[at, ci:] = p[prow:]
    preact = dot(act[:m], wk[0], 1, 0)
    for k in range(1, taps):
        preact = preact + dot(act[k * SPAN : k * SPAN + m], wk[k], 1, 0)
    hidden, slope = gelu_both(preact)
    upstream = dot(wide[...], wp_s[...].astype(BF16), 1, 1)
    deltas = (upstream * slope).astype(BF16)
    delta[...] = deltas
    inner = deltas[SPAN : SPAN + n]

    def place(v, at, pieces):
        count = v.shape[0] // (2 * groups)
        for core in range(2):

            @pl.when(c == core)
            def _():
                for i in range(groups):
                    own, other = (2 * i + core) * count, (2 * i + 1 - core) * count
                    mine[i, at : at + pieces * count] = halves(v[own : own + count], pieces)
                    send[i, at : at + pieces * count] = halves(v[other : other + count], pieces).astype(BF16)

    place(dot(hidden[SPAN : SPAN + n].astype(BF16), wide[SPAN : SPAN + n], 0, 0), taps * rows, 2)
    for k in range(taps):
        place(dot(act[(k + 1) * SPAN : (k + 1) * SPAN + n], inner, 0, 0), k * rows, 1)


def halves(v, pieces):
    width = v.shape[1] // pieces
    return jnp.concatenate([v[:, k * width : (k + 1) * width] for k in range(pieces)], axis=0)


def spread_body(parts, copies):
    total = jnp.sum(parts[...].astype(F32), axis=0)
    for i in range(copies.shape[0]):
        copies[i] = total


def finish_body(s, conv, point):
    taps, rows, ci = conv.shape
    for k in range(taps):
        conv[k] = s[k * rows : (k + 1) * rows]
    q, prow = taps * rows, point.shape[0]
    point[:, :ci] = s[q : q + prow]
    point[:, ci:] = s[q + prow :]


def input_body(delta, wk, _, x, cot, out):
    taps, n = wk.shape[0], x.shape[0]
    grad = dot(delta[(taps - 1) * SPAN : (taps - 1) * SPAN + n], wk[0], 1, 1)
    for k in range(1, taps):
        at = (taps - 1 - k) * SPAN
        grad = grad + dot(delta[at : at + n], wk[k], 1, 1)
    v = x[...].astype(F32)
    r = inverse_rms(v)
    _, slope = gelu_both(v * r)
    g = grad * slope
    inner = r * g - v * (r * r * r * jnp.mean(v * g, axis=-1, keepdims=True))
    out[...] = (cot[...].astype(F32) + inner).astype(BF16)


def sds(shape, dtype):
    return jax.ShapeDtypeStruct(shape, dtype)


def in_hbm(a):
    return pltpu.with_memory_space_constraint(a, pltpu.HBM)


def limit(mib):
    return pltpu.CompilerParams(vmem_limit_bytes=mib << 20)


def exchanged_sum(x, axis):
    n = lax.axis_size(axis)
    y = lax.all_to_all(x, axis, 0, 0, tiled=True)
    return jnp.sum(y.reshape((n, x.shape[0] // n) + x.shape[1:]).astype(F32), axis=0)


def per_device(inputs, cotangent, dilated_kernel_weight, point_weight):
    x, cot = inputs[0], cotangent[0]
    n, C = x.shape
    rows, taps, CI = dilated_kernel_weight.shape
    prow = point_weight.shape[0]
    total = taps * rows + 2 * prow
    groups = lax.axis_size("xl") * lax.axis_size("y")
    seq = lax.axis_size(SEQ)
    core = lax.axis_index("c")
    h = 2 * SPAN
    whole = lambda *s: pl.BlockSpec(s, lambda *_: (0,) * len(s))

    last = n // h - 1
    edge = n // SPAN - 1
    copies, up, down = pl.pallas_call(
        pack_body,
        grid=(1,),
        in_specs=[
            whole(taps, rows, CI),
            whole(prow, C),
            pl.BlockSpec((h, C), lambda i: (0, 0)),
            pl.BlockSpec((h, C), lambda i: (last, 0)),
            pl.BlockSpec((SPAN, C), lambda i: (0, 0)),
            pl.BlockSpec((SPAN, C), lambda i: (edge, 0)),
        ],
        out_specs=[whole(groups, total, CI), whole(h + SPAN, C), whole(h + SPAN, C)],
        out_shape=[sds((groups, total, CI), BF16), sds((h + SPAN, C), BF16), sds((h + SPAN, C), BF16)],
        name="pack",
        compiler_params=limit(2),
    )(*map(in_hbm, (jnp.swapaxes(dilated_kernel_weight, 0, 1), point_weight, x, x, cot, cot)))

    after = lax.ppermute(down, SEQ, [(i + 1, i) for i in range(seq - 1)])
    before = lax.ppermute(up, SEQ, [(i, i + 1) for i in range(seq - 1)])
    near = lax.all_to_all(copies.reshape(groups * total, CI), ("xl", "y"), 0, 0, tiled=True)
    far = lax.ppermute(near, "c", PAIR)
    near, far = near.reshape(groups, total, CI), far.reshape(groups, total, CI)

    spec = pl.BlockSpec(memory_space=pltpu.VMEM)
    tile = pl.BlockSpec((16, 128), lambda i: (0, 0))
    mark = pl.pallas_call(
        settle_body,
        grid=(1,),
        in_specs=[tile] * 2,
        out_specs=tile,
        out_shape=sds((16, 128), F32),
        name="settle",
        compiler_params=limit(2),
    )(before, after)
    act, wide = pl.pallas_call(
        act_body,
        in_specs=[spec] * 5,
        out_specs=[spec] * 2,
        out_shape=[sds((n + 2 * h, C), BF16), sds((n + h, C), BF16)],
        name="act",
        compiler_params=limit(2),
    )(mark, x, cot, before, after)
    delta, wk, mine, send, spare = pl.pallas_call(
        main_body,
        in_specs=[pl.BlockSpec(memory_space=pltpu.SMEM)] + [spec] * 4,
        out_specs=[spec] * 5,
        out_shape=[
            sds((n + h, CI), BF16),
            sds((taps, C, CI), BF16),
            sds((groups, total, CI), F32),
            sds((groups, total, CI), BF16),
            sds((CI, C), F32),
        ],
        name="main",
        compiler_params=limit(2),
    )(core.reshape(1).astype(jnp.int32), near, far, act, wide)
    got = lax.ppermute(send, "c", PAIR)
    grad_input = pl.pallas_call(input_body, in_specs=[spec] * 5, out_shape=sds((n, C), BF16), name="input_grad", compiler_params=limit(2))(delta, wk, spare, x, cot)

    s = (mine + got.astype(F32)).astype(BF16).reshape(groups * total, CI)
    s = exchanged_sum(s, ("xl", "y", "xh", "zl"))
    parts = lax.all_gather(s.astype(BF16), "zh", axis=0)
    final = lax.axis_size("xh") * lax.axis_size("zl")
    own = s.shape[0]
    s = pl.pallas_call(
        spread_body,
        in_specs=[spec],
        out_specs=spec,
        out_shape=sds((final, own, CI), F32),
        name="spread",
        compiler_params=limit(2),
    )(parts)
    s = lax.all_to_all(s.reshape(final * own, CI), ("xh", "zl"), 0, 0, tiled=True)
    conv, owned_point = pl.pallas_call(
        finish_body,
        in_specs=[spec],
        out_specs=[spec] * 2,
        out_shape=[sds((taps, rows, CI), F32), sds((prow, C), F32)],
        name="finish",
        compiler_params=limit(2),
    )(s)
    owned_conv = jnp.swapaxes(conv, 0, 1)
    return (grad_input[None], owned_conv, owned_point)


def solution(mesh):
    fine = Mesh(mesh.devices.reshape(2, 4, 2, 2, 32 // ZL, ZL), DP + SEQ)
    return jax.shard_map(
        per_device,
        mesh=fine,
        in_specs=(P(DP, SEQ, None), P(DP, SEQ, None), P(DP, None, None), P(DP, None)),
        out_specs=(P(DP, SEQ, None), P(DP, None, None), P(DP, None)),
        check_vma=False,
    )
```

```python
import jax
import jax.numpy as jnp
from jax import lax
from jax.experimental import pallas as pl
from jax.experimental.pallas import tpu as pltpu
from jax.sharding import Mesh
from jax.sharding import PartitionSpec as P


SPAN = 32
EPS = 1e-06
ALPHA = 0.7978845608028654
BETA = 0.044715
ZL = 2
DP = ("xl", "y", "c")
SEQ = ("xh", "zh", "zl")
PAIR = [(0, 1), (1, 0)]
BF16, F32 = jnp.bfloat16, jnp.float32


def dot(a, b, ca, cb):
    return lax.dot_general(a, b, (((ca,), (cb,)), ((), ())), preferred_element_type=F32)


def gelu_value(v):
    return 0.5 * v * (1.0 + jnp.tanh(ALPHA * (v + BETA * (v * v * v))))


def gelu_both(v):
    t = jnp.tanh(ALPHA * (v + BETA * (v * v * v)))
    half = 0.5 * (1.0 + t)
    slope = half + 0.5 * v * (1.0 - t * t) * (ALPHA * (1.0 + 3.0 * BETA * (v * v)))
    return v * half, slope


def inverse_rms(x):
    return lax.rsqrt(jnp.mean(x * x, axis=-1, keepdims=True) + EPS)


def pack_body(wk, wp, xa, xb, ca, cb, copies, up, down, tile, sems):
    taps, rows, _ = wk.shape
    for k in range(taps):
        tile[k * rows : (k + 1) * rows] = wk[k]
    tile[taps * rows :] = halves(wp[...].astype(F32), 2).astype(BF16)
    sends = [pltpu.make_async_copy(tile, copies.at[i], sems.at[i]) for i in range(copies.shape[0])]
    for send in sends:
        send.start()
    up[: 2 * SPAN] = xb[...]
    up[2 * SPAN :] = cb[...]
    down[: 2 * SPAN] = xa[...]
    down[2 * SPAN :] = ca[...]
    for send in sends:
        send.wait()


def settle_body(before, after, mark):
    mark[...] = before[...].astype(F32) + after[...].astype(F32)


def act_body(_, x, cot, before, after, act, wide):
    n, h = x.shape[0], 2 * SPAN

    def part(v):
        v = v.astype(F32)
        return gelu_value(v * inverse_rms(v)).astype(BF16)

    act[:h] = part(before[:h])
    act[h : h + n] = part(x[...])
    act[h + n :] = part(after[:h])
    wide[:SPAN] = before[h:]
    wide[SPAN : SPAN + n] = cot[...]
    wide[SPAN + n :] = after[h:]


def main_body(c_ref, near, far, act, wide, delta, wk, mine, send, wp_s):
    c = c_ref[0]
    groups, _, ci = near.shape
    taps, channels, _ = wk.shape
    rows, prow = channels // (2 * groups), ci // (2 * groups)
    m = wide.shape[0]
    n = m - 2 * SPAN
    for ref, core in ((near, c), (far, 1 - c)):
        for i in range(groups):
            d = 2 * i + core
            for k in range(taps):
                wk[k, pl.ds(pl.multiple_of(d * rows, rows), rows)] = ref[i, k * rows : (k + 1) * rows]
            p = ref[i, taps * rows :].astype(F32)
            at = pl.ds(pl.multiple_of(d * prow, prow), prow)
            wp_s[at, :ci] = p[:prow]
            wp_s[at, ci:] = p[prow:]
    preact = dot(act[:m], wk[0], 1, 0)
    for k in range(1, taps):
        preact = preact + dot(act[k * SPAN : k * SPAN + m], wk[k], 1, 0)
    hidden, slope = gelu_both(preact)
    upstream = dot(wide[...], wp_s[...].astype(BF16), 1, 1)
    deltas = (upstream * slope).astype(BF16)
    delta[...] = deltas
    inner = deltas[SPAN : SPAN + n]

    def place(v, at, pieces):
        count = v.shape[0] // (2 * groups)
        for core in range(2):

            @pl.when(c == core)
            def _():
                for i in range(groups):
                    own, other = (2 * i + core) * count, (2 * i + 1 - core) * count
                    mine[i, at : at + pieces * count] = halves(v[own : own + count], pieces)
                    send[i, at : at + pieces * count] = halves(v[other : other + count], pieces).astype(BF16)

    place(dot(hidden[SPAN : SPAN + n].astype(BF16), wide[SPAN : SPAN + n], 0, 0), taps * rows, 2)
    for k in range(taps):
        place(dot(act[(k + 1) * SPAN : (k + 1) * SPAN + n], inner, 0, 0), k * rows, 1)


def halves(v, pieces):
    width = v.shape[1] // pieces
    return jnp.concatenate([v[:, k * width : (k + 1) * width] for k in range(pieces)], axis=0)


def spread_body(parts, copies):
    total = jnp.sum(parts[...].astype(F32), axis=0)
    for i in range(copies.shape[0]):
        copies[i] = total


def finish_body(s, conv, point):
    taps, rows, ci = conv.shape
    for k in range(taps):
        conv[k] = s[k * rows : (k + 1) * rows]
    q, prow = taps * rows, point.shape[0]
    point[:, :ci] = s[q : q + prow]
    point[:, ci:] = s[q + prow :]


def input_body(delta, wk, _, x, cot, out):
    taps, n = wk.shape[0], x.shape[0]
    grad = dot(delta[(taps - 1) * SPAN : (taps - 1) * SPAN + n], wk[0], 1, 1)
    for k in range(1, taps):
        at = (taps - 1 - k) * SPAN
        grad = grad + dot(delta[at : at + n], wk[k], 1, 1)
    v = x[...].astype(F32)
    r = inverse_rms(v)
    _, slope = gelu_both(v * r)
    g = grad * slope
    inner = r * g - v * (r * r * r * jnp.mean(v * g, axis=-1, keepdims=True))
    out[...] = (cot[...].astype(F32) + inner).astype(BF16)


def sds(shape, dtype):
    return jax.ShapeDtypeStruct(shape, dtype)


def in_hbm(a):
    return pltpu.with_memory_space_constraint(a, pltpu.HBM)


def limit(mib):
    return pltpu.CompilerParams(vmem_limit_bytes=mib << 20)


def exchanged_sum(x, axis):
    n = lax.axis_size(axis)
    y = lax.all_to_all(x, axis, 0, 0, tiled=True)
    return jnp.sum(y.reshape((n, x.shape[0] // n) + x.shape[1:]).astype(F32), axis=0)


def per_device(inputs, cotangent, dilated_kernel_weight, point_weight):
    x, cot = inputs[0], cotangent[0]
    n, C = x.shape
    rows, taps, CI = dilated_kernel_weight.shape
    prow = point_weight.shape[0]
    total = taps * rows + 2 * prow
    groups = lax.axis_size("xl") * lax.axis_size("y")
    seq = lax.axis_size(SEQ)
    core = lax.axis_index("c")
    h = 2 * SPAN
    whole = lambda *s: pl.BlockSpec(s, lambda *_: (0,) * len(s))

    last = n // h - 1
    edge = n // SPAN - 1
    copies, up, down = pl.pallas_call(
        pack_body,
        grid=(1,),
        in_specs=[
            whole(taps, rows, CI),
            whole(prow, C),
            pl.BlockSpec((h, C), lambda i: (0, 0)),
            pl.BlockSpec((h, C), lambda i: (last, 0)),
            pl.BlockSpec((SPAN, C), lambda i: (0, 0)),
            pl.BlockSpec((SPAN, C), lambda i: (edge, 0)),
        ],
        out_specs=[pl.BlockSpec(memory_space=pltpu.HBM), whole(h + SPAN, C), whole(h + SPAN, C)],
        out_shape=[sds((groups, total, CI), BF16), sds((h + SPAN, C), BF16), sds((h + SPAN, C), BF16)],
        scratch_shapes=[pltpu.VMEM((total, CI), BF16), pltpu.SemaphoreType.DMA((groups,))],
        name="pack",
        compiler_params=limit(2),
    )(*map(in_hbm, (jnp.swapaxes(dilated_kernel_weight, 0, 1), point_weight, x, x, cot, cot)))

    after = lax.ppermute(down, SEQ, [(i + 1, i) for i in range(seq - 1)])
    before = lax.ppermute(up, SEQ, [(i, i + 1) for i in range(seq - 1)])
    near = lax.all_to_all(copies.reshape(groups * total, CI), ("xl", "y"), 0, 0, tiled=True)
    far = lax.ppermute(near, "c", PAIR)
    near, far = near.reshape(groups, total, CI), far.reshape(groups, total, CI)

    spec = pl.BlockSpec(memory_space=pltpu.VMEM)
    tile = pl.BlockSpec((16, 128), lambda i: (0, 0))
    mark = pl.pallas_call(
        settle_body,
        grid=(1,),
        in_specs=[tile] * 2,
        out_specs=tile,
        out_shape=sds((16, 128), F32),
        name="settle",
        compiler_params=limit(2),
    )(before, after)
    act, wide = pl.pallas_call(
        act_body,
        in_specs=[spec] * 5,
        out_specs=[spec] * 2,
        out_shape=[sds((n + 2 * h, C), BF16), sds((n + h, C), BF16)],
        name="act",
        compiler_params=limit(2),
    )(mark, x, cot, before, after)
    delta, wk, mine, send, spare = pl.pallas_call(
        main_body,
        in_specs=[pl.BlockSpec(memory_space=pltpu.SMEM)] + [spec] * 4,
        out_specs=[spec] * 5,
        out_shape=[
            sds((n + h, CI), BF16),
            sds((taps, C, CI), BF16),
            sds((groups, total, CI), F32),
            sds((groups, total, CI), BF16),
            sds((CI, C), F32),
        ],
        name="main",
        compiler_params=limit(2),
    )(core.reshape(1).astype(jnp.int32), near, far, act, wide)
    got = lax.ppermute(send, "c", PAIR)
    grad_input = pl.pallas_call(input_body, in_specs=[spec] * 5, out_shape=sds((n, C), BF16), name="input_grad", compiler_params=limit(2))(delta, wk, spare, x, cot)

    s = (mine + got.astype(F32)).astype(BF16).reshape(groups * total, CI)
    s = exchanged_sum(s, ("xl", "y", "xh", "zl"))
    parts = lax.all_gather(s.astype(BF16), "zh", axis=0)
    final = lax.axis_size("xh") * lax.axis_size("zl")
    own = s.shape[0]
    s = pl.pallas_call(
        spread_body,
        in_specs=[spec],
        out_specs=spec,
        out_shape=sds((final, own, CI), F32),
        name="spread",
        compiler_params=limit(2),
    )(parts)
    s = lax.all_to_all(s.reshape(final * own, CI), ("xh", "zl"), 0, 0, tiled=True)
    conv, owned_point = pl.pallas_call(
        finish_body,
        in_specs=[spec],
        out_specs=[spec] * 2,
        out_shape=[sds((taps, rows, CI), F32), sds((prow, C), F32)],
        name="finish",
        compiler_params=limit(2),
    )(s)
    owned_conv = jnp.swapaxes(conv, 0, 1)
    return (grad_input[None], owned_conv, owned_point)


def solution(mesh):
    fine = Mesh(mesh.devices.reshape(2, 4, 2, 2, 32 // ZL, ZL), DP + SEQ)
    return jax.shard_map(
        per_device,
        mesh=fine,
        in_specs=(P(DP, SEQ, None), P(DP, SEQ, None), P(DP, None, None), P(DP, None)),
        out_specs=(P(DP, SEQ, None), P(DP, None, None), P(DP, None)),
        check_vma=False,
    )
```
